32 devices in a mesh: groups: 2 (over x), blk: 4 (over y, core), ref: 4 (over z).
Axes of the slice: x: 2, y: 2, z: 4, core: 2. Of those that a mesh axis runs over, the one named last changes fastest.
Arguments:
- queries: bfloat16 [4096, 1024], P(('groups', 'blk')), parts along dimension 0, may hold values from -4 to 4
- references: bfloat16 [8192, 1024], P(('groups', 'blk', 'ref')), parts along dimension 0, may hold values from -4 to 4
- labels: bfloat16 [8192, 512], P(('groups', 'blk', 'ref')), parts along dimension 0, may hold values from 0.0009994507 to 1
Outputs:
- log_scores: float32 [4096, 512], P(('groups', 'blk', 'ref')), parts along dimension 0
The draws below stay inside these ranges and needn't reach their ends.
There are 2 independent parts, one for each index of `groups`. The reference program is written for one: setup_inputs(seed, part) draws one part's arguments, and reference() takes and returns one part's arrays. A program takes and returns all parts, laid end to end along the dimension named above; each array names one. Nothing has to cross between parts.
All inputs are finite; a program needn't handle non-finite values.
Results may differ from the reference program's by a relative error of at most 0.007.
Values may be sent and summed in bfloat16 or wider, within the bound.
No kernel may reach another device: no remote copies, remote signals or barrier semaphores. Data moves between devices by JAX's collectives and lax.ppermute only.
A program may use at most 128 MiB of HBM per device.

```python
import math
import jax
import jax.numpy as jnp
from jax import lax

E = 1024
C = 512
Q_DEV = 512
NQ = 2048
NR = 4096


def draw_pair(key):
    base_key = jax.random.fold_in(key, 7)
    subkeys = jax.random.split(base_key, 2)
    queries = jnp.clip(jax.random.normal(subkeys[0], (NQ, E), jnp.float32), -4.0, 4.0)
    references = jnp.clip(jax.random.normal(subkeys[1], (NR, E), jnp.float32), -4.0, 4.0)
    return (queries.astype(jnp.bfloat16), references.astype(jnp.bfloat16))


def draw_queries(key, part):
    return draw_pair(key)[0]


def draw_references(key, part):
    return draw_pair(key)[1]


def level_of(stream_key, extent, cuts, least, top_value):
    loudness = 1.0
    for position, parts in cuts:
        steps = jax.random.uniform(jax.random.fold_in(jax.random.fold_in(stream_key, 6), position), (parts,), jnp.float32, least / len(cuts), top_value / len(cuts))
        loudness = loudness * jnp.repeat(jnp.exp(steps), extent[position] // parts).reshape((-1,) + (1,) * (len(extent) - 1 - position))
    return loudness


def setup_inputs(seed: int = 0, part: int = 0) -> dict:
    keys = jax.random.split(jax.random.key(seed), 4)
    own_keys = jax.random.split(jax.random.fold_in(keys[3], part), 4)
    return {
        "queries": draw_queries(jax.random.fold_in(jax.random.fold_in(keys[3], part), 71), part),
        "references": draw_references(jax.random.fold_in(jax.random.fold_in(keys[3], part), 71), part),
        "labels": jnp.clip(jnp.exp(math.log(1.0) - 6.9083047 * jax.random.uniform(own_keys[2], (NR, C), jnp.float32) ** level_of(own_keys[2], (NR, C), ((0, 16),), -0.2, 0.2)), 0.0009994507, 1.0).astype(jnp.bfloat16),
    }


def reference(queries, references, labels):
    width = queries.shape[1]
    classes = labels.shape[1]
    score_scale = 2.0 / math.sqrt(width)
    blocked = queries.reshape(NQ // Q_DEV, Q_DEV, width)

    def one_block(members):
        scores = jnp.dot(members, references.T, preferred_element_type=jnp.float32) * score_scale
        row_top = lax.optimization_barrier(jnp.max(scores, axis=1))
        weights = jnp.exp(scores - row_top[:, None]).astype(jnp.bfloat16)
        row_total = lax.optimization_barrier(jnp.sum(weights.astype(jnp.float32), axis=1))
        row_mass = jnp.dot(weights, labels, preferred_element_type=jnp.float32)
        return jnp.log(row_mass) - jnp.log(row_total)[:, None]
    return lax.map(one_block, blocked).reshape(NQ, classes)
```

```python
import math

import jax
import jax.numpy as jnp
from jax import lax
from jax.experimental import pallas as pl
from jax.experimental.pallas import tpu as pltpu
from jax.sharding import PartitionSpec as P

NEG_FLOOR = -1e30


def merged(value, axis, join):
    pieces = jax.tree.map(lambda part: lax.all_gather(part, axis), value)
    head = jax.tree.map(lambda part: part[0], pieces)
    tail = jax.tree.map(lambda part: part[1:], pieces)
    subtotal, _ = lax.scan(lambda subtotal, piece: (join(subtotal, piece), None), head, tail)
    return subtotal


def absorb(running, queries, ref_rows, label_rows, score_scale):
    row_top, row_total, row_mass = running
    scores = (
        lax.dot_general(
            queries, ref_rows, (((1,), (1,)), ((), ())), preferred_element_type=jnp.float32
        )
        * score_scale
    )
    new_top = jnp.maximum(row_top, jnp.max(scores, axis=1))
    shrink = jnp.exp(row_top - new_top)
    weights = jnp.exp(scores - new_top[:, None]).astype(jnp.bfloat16)
    row_total = row_total * shrink + jnp.sum(weights.astype(jnp.float32), axis=1)
    row_mass = row_mass * shrink[:, None] + jnp.dot(
        weights, label_rows, preferred_element_type=jnp.float32
    )
    return (new_top, row_total, row_mass)


def combine(first, second):
    new_top = jnp.maximum(first[0], second[0])
    scale_first = jnp.exp(first[0] - new_top)
    scale_second = jnp.exp(second[0] - new_top)
    row_total = first[1] * scale_first + second[1] * scale_second
    row_mass = first[2] * scale_first[:, None] + second[2] * scale_second[:, None]
    return (new_top, row_total, row_mass)


def plain(queries, references, labels):
    width = queries.shape[1]
    classes = labels.shape[1]
    query_rows = queries.shape[0]
    score_scale = 2.0 / math.sqrt(width)
    initial = (
        jnp.full((query_rows,), NEG_FLOOR, jnp.float32),
        jnp.zeros((query_rows,), jnp.float32),
        jnp.zeros((query_rows, classes), jnp.float32),
    )
    running = initial
    ref_part = lax.all_gather(references, "blk", axis=0, tiled=True)
    label_part = lax.all_gather(labels, "blk", axis=0, tiled=True)
    count = ref_part.shape[0]
    span = math.gcd(count, 512)
    grouped_refs = ref_part.reshape(count // span, span, width)
    grouped_labels = label_part.reshape(count // span, span, classes)

    def advance(current, members):
        return (absorb(current, queries, members[0], members[1], score_scale), None)

    running, unused = lax.scan(advance, running, (grouped_refs, grouped_labels))
    row_top, row_total, row_mass = running
    share = query_rows // lax.axis_size("ref")
    row_top, row_total, row_mass = merged((row_top, row_total, row_mass), "ref", combine)
    offset = lax.axis_index("ref") * share
    mass_rows = lax.dynamic_slice_in_dim(row_mass, offset, share, 0)
    total_rows = lax.dynamic_slice_in_dim(row_total, offset, share, 0)
    return jnp.log(mass_rows) - jnp.log(total_rows)[:, None]


LANES = 128
STAT_ROWS = 16
GRANT = 24 << 20
BF16 = jnp.bfloat16
F32 = jnp.float32
VMEM = pl.BlockSpec(memory_space=pltpu.VMEM)
SMEM = pl.BlockSpec(memory_space=pltpu.SMEM)


def call(kernel, outs, in_specs, flops, name):
    shapes = [jax.ShapeDtypeStruct(shape, dtype) for shape, dtype in outs]
    moved = sum(math.prod(shape) * jnp.dtype(dtype).itemsize for shape, dtype in outs)
    return pl.pallas_call(
        kernel,
        out_shape=shapes,
        in_specs=in_specs,
        out_specs=[VMEM] * len(shapes),
        cost_estimate=pl.CostEstimate(flops=flops, bytes_accessed=moved, transcendentals=0),
        compiler_params=pltpu.CompilerParams(vmem_limit_bytes=GRANT),
        name=name,
    )


def swapped(value, axis, bit):
    return lax.ppermute(value, axis, [(i, i ^ bit) for i in range(lax.axis_size(axis))])


def scored(ref_rows, queries):
    scale = 2.0 / math.sqrt(queries.shape[1])
    return (
        lax.dot_general(
            ref_rows, queries, (((1,), (1,)), ((), ())), preferred_element_type=F32
        )
        * scale
    )


def even_top(top):
    return top.astype(BF16).astype(F32)


def arrange_kernel(place_ref, queries_ref, labels_ref, ordered_ref, upper_ref, lower_ref):
    share = LANES
    place = place_ref[0]
    for block in range(queries_ref.shape[0] // share):
        first = pl.multiple_of((place ^ block) * share, share)
        ordered_ref[block * share : (block + 1) * share, :] = queries_ref[pl.ds(first, share), :]
    half = labels_ref.shape[1] // 2
    upper_ref[...] = labels_ref[:, :half].T
    lower_ref[...] = labels_ref[:, half:].T


def own_kernel(queries_ref, refs_a, refs_b, up_a, up_b, low_a, low_b, upper_ref, lower_ref, stat_ref):
    queries = queries_ref[...]
    scores_a = scored(refs_a[...], queries)
    scores_b = scored(refs_b[...], queries)
    top = jnp.maximum(
        jnp.max(scores_a, axis=0, keepdims=True), jnp.max(scores_b, axis=0, keepdims=True)
    )
    top = even_top(top)
    weights_a = jnp.exp(scores_a - top).astype(BF16)
    weights_b = jnp.exp(scores_b - top).astype(BF16)
    total = jnp.sum(weights_a.astype(F32), axis=0, keepdims=True) + jnp.sum(
        weights_b.astype(F32), axis=0, keepdims=True
    )
    for out, first, second in ((upper_ref, up_a, up_b), (lower_ref, low_a, low_b)):
        out[...] = jnp.dot(first[...], weights_a, preferred_element_type=F32) + jnp.dot(
            second[...], weights_b, preferred_element_type=F32
        )
    stat_ref[0:1, :] = top
    stat_ref[1:2, :] = total


def score_kernel(queries_ref, refs_ref, scores_ref):
    scores_ref[...] = scored(refs_ref[...], queries_ref[...])


def weight_kernel(queries_ref, refs_ref, scores_ref, stat_ref, weights_ref, out_ref):
    scores_a = scores_ref[...]
    scores_b = scored(refs_ref[...], queries_ref[...])
    rows = scores_a.shape[0]
    top = jnp.maximum(
        jnp.max(scores_a, axis=0, keepdims=True), jnp.max(scores_b, axis=0, keepdims=True)
    )
    own_top = stat_ref[0:1, :]
    top = jnp.maximum(even_top(top), own_top)
    weights_a = jnp.exp(scores_a - top).astype(BF16)
    weights_b = jnp.exp(scores_b - top).astype(BF16)
    weights_ref[:rows, :] = weights_a
    weights_ref[rows:, :] = weights_b
    shrink = jnp.exp(own_top - top)
    total = (
        stat_ref[1:2, :] * shrink
        + jnp.sum(weights_a.astype(F32), axis=0, keepdims=True)
        + jnp.sum(weights_b.astype(F32), axis=0, keepdims=True)
    )
    out_ref[0:1, :] = top
    out_ref[1:2, :] = total
    out_ref[2:3, :] = shrink


def write_message(message_ref, columns, mass, top, total):
    height = mass.shape[0]
    high = total.astype(BF16)
    low = (total - high.astype(F32)).astype(BF16)
    message_ref[:height, columns] = mass.astype(BF16)
    row = lax.broadcasted_iota(jnp.int32, (STAT_ROWS, mass.shape[1]), 0)
    stats = jnp.where(
        row == 0, top, jnp.where(row == 1, high.astype(F32), low.astype(F32))
    )
    message_ref[height:, columns] = stats.astype(BF16)


def read_message(message_ref, columns):
    height = message_ref.shape[0] - STAT_ROWS
    mass = message_ref[:height, columns].astype(F32)
    stats = message_ref[height:, columns].astype(F32)
    return mass, stats[0:1], stats[1:2] + stats[2:3]


def mass_kernel(label_a, label_b, weights_ref, own_ref, stat_ref, message_ref, keep_ref):
    rows = label_a.shape[1]
    mass = (
        own_ref[...] * stat_ref[2:3, :]
        + jnp.dot(label_a[...], weights_ref[:rows, :], preferred_element_type=F32)
        + jnp.dot(label_b[...], weights_ref[rows:, :], preferred_element_type=F32)
    )
    for slot in range(2):
        columns = slice(slot * LANES, (slot + 1) * LANES)
        kept = slice(2 * slot * LANES, (2 * slot + 1) * LANES)
        sent = slice((2 * slot + 1) * LANES, (2 * slot + 2) * LANES)
        write_message(
            message_ref, columns, mass[:, sent], stat_ref[0:1, sent], stat_ref[1:2, sent]
        )
        keep_ref[:, columns] = mass[:, kept]


def joined(mass, top, total, other):
    other_mass, other_top, other_total = other
    new_top = jnp.maximum(top, other_top)
    scale = jnp.exp(top - new_top)
    other_scale = jnp.exp(other_top - new_top)
    return (
        mass * scale + other_mass * other_scale,
        new_top,
        total * scale + other_total * other_scale,
    )


def halve_kernel(received_ref, keep_ref, stat_ref, message_ref, out_ref, out_stat_ref):
    near, far = slice(0, LANES), slice(LANES, 2 * LANES)
    block = slice(2 * LANES, 3 * LANES)
    mass, top, total = joined(
        keep_ref[:, far], stat_ref[0:1, block], stat_ref[1:2, block], read_message(received_ref, far)
    )
    write_message(message_ref, slice(None), mass, top, total)
    mass, top, total = joined(
        keep_ref[:, near], stat_ref[0:1, near], stat_ref[1:2, near], read_message(received_ref, near)
    )
    out_ref[...] = mass
    out_stat_ref[0:1, :] = top
    out_stat_ref[1:2, :] = total


def final_kernel(got_upper, got_lower, upper_ref, lower_ref, stat_ref, out_ref):
    half = upper_ref.shape[0]
    for part, (got, keep) in enumerate(((got_upper, upper_ref), (got_lower, lower_ref))):
        mass, _, total = joined(
            keep[...], stat_ref[0:1, :], stat_ref[1:2, :], read_message(got, slice(None))
        )
        out_ref[:, part * half : (part + 1) * half] = (jnp.log(mass) - jnp.log(total)).T


def fits(queries, references, labels):
    share = queries.shape[0] // lax.axis_size("ref")
    return (
        lax.axis_size("blk") == 4
        and lax.axis_size("ref") == 4
        and share == LANES
        and labels.shape[1] % (2 * LANES) == 0
        and references.shape[0] % LANES == 0
    )


def per_device(queries, references, labels):
    if not fits(queries, references, labels):
        return plain(queries, references, labels)
    count, width = references.shape
    rows, classes = queries.shape[0], labels.shape[1]
    half = classes // 2
    pair = 2 * LANES
    score_flops = 2 * count * rows * width
    mass_flops = 4 * count * rows * half

    far_refs = swapped(references, "blk", 2)
    mate_refs = swapped(references, "blk", 1)
    place = lax.axis_index("ref").astype(jnp.int32).reshape(1)
    ordered, upper, lower = call(
        arrange_kernel,
        [((rows, width), BF16), ((half, count), BF16), ((half, count), BF16)],
        [SMEM, VMEM, VMEM],
        0,
        "arrange",
    )(place, queries, labels)
    far_labels = [swapped(part, "blk", 2) for part in (upper, lower)]
    mate_labels = [swapped(part, "blk", 1) for part in (upper, lower)]
    own_upper, own_lower, own_stat = call(
        own_kernel,
        [((half, rows), F32), ((half, rows), F32), ((8, rows), F32)],
        [VMEM] * 7,
        2 * score_flops + 2 * mass_flops,
        "own",
    )(ordered, references, mate_refs, upper, mate_labels[0], lower, mate_labels[1])
    cross_refs = swapped(far_refs, "blk", 1)
    cross_labels = [swapped(part, "blk", 1) for part in far_labels]
    (scores,) = call(
        score_kernel, [((count, rows), F32)], [VMEM] * 2, score_flops, "score"
    )(ordered, far_refs)
    weights, stat = call(
        weight_kernel,
        [((2 * count, rows), BF16), ((8, rows), F32)],
        [VMEM] * 4,
        score_flops,
        "weight",
    )(ordered, cross_refs, scores, own_stat)
    got, kept = [], []
    for own, far, cross in zip((own_upper, own_lower), far_labels, cross_labels):
        message, keep = call(
            mass_kernel,
            [((half + STAT_ROWS, pair), BF16), ((half, pair), F32)],
            [VMEM] * 5,
            mass_flops,
            "mass",
        )(far, cross, weights, own, stat)
        received = swapped(message, "ref", 1)
        message, keep, near_stat = call(
            halve_kernel,
            [((half + STAT_ROWS, LANES), BF16), ((half, LANES), F32), ((8, LANES), F32)],
            [VMEM] * 3,
            0,
            "halve",
        )(received, keep, stat)
        got.append(swapped(message, "ref", 2))
        kept.append(keep)
    (out,) = call(final_kernel, [((LANES, classes), F32)], [VMEM] * 5, 0, "final")(
        *got, *kept, near_stat
    )
    return out


def solution(mesh):
    return jax.shard_map(
        per_device,
        mesh=mesh,
        in_specs=(
            P(("groups", "blk"), None),
            P(("groups", "blk", "ref"), None),
            P(("groups", "blk", "ref"), None),
        ),
        out_specs=P(("groups", "blk", "ref"), None),
        check_vma=False,
    )
```

```python
import functools
import math

import jax
import jax.numpy as jnp
from jax import lax
from jax.experimental import pallas as pl
from jax.experimental.pallas import tpu as pltpu
from jax.sharding import PartitionSpec as P


NEG_FLOOR = -1e30


def merged(value, axis, join):
    pieces = jax.tree.map(lambda part: lax.all_gather(part, axis), value)
    head = jax.tree.map(lambda part: part[0], pieces)
    tail = jax.tree.map(lambda part: part[1:], pieces)
    subtotal, _ = lax.scan(lambda subtotal, piece: (join(subtotal, piece), None), head, tail)
    return subtotal


def absorb(running, queries, ref_rows, label_rows, score_scale):
    row_top, row_total, row_mass = running
    scores = (
        lax.dot_general(
            queries, ref_rows, (((1,), (1,)), ((), ())), preferred_element_type=jnp.float32
        )
        * score_scale
    )
    new_top = jnp.maximum(row_top, jnp.max(scores, axis=1))
    shrink = jnp.exp(row_top - new_top)
    weights = jnp.exp(scores - new_top[:, None]).astype(jnp.bfloat16)
    row_total = row_total * shrink + jnp.sum(weights.astype(jnp.float32), axis=1)
    row_mass = row_mass * shrink[:, None] + jnp.dot(
        weights, label_rows, preferred_element_type=jnp.float32
    )
    return (new_top, row_total, row_mass)


def combine(first, second):
    new_top = jnp.maximum(first[0], second[0])
    scale_first = jnp.exp(first[0] - new_top)
    scale_second = jnp.exp(second[0] - new_top)
    row_total = first[1] * scale_first + second[1] * scale_second
    row_mass = first[2] * scale_first[:, None] + second[2] * scale_second[:, None]
    return (new_top, row_total, row_mass)


def plain(queries, references, labels):
    width = queries.shape[1]
    classes = labels.shape[1]
    query_rows = queries.shape[0]
    score_scale = 2.0 / math.sqrt(width)
    initial = (
        jnp.full((query_rows,), NEG_FLOOR, jnp.float32),
        jnp.zeros((query_rows,), jnp.float32),
        jnp.zeros((query_rows, classes), jnp.float32),
    )
    running = initial
    ref_part = lax.all_gather(references, "blk", axis=0, tiled=True)
    label_part = lax.all_gather(labels, "blk", axis=0, tiled=True)
    count = ref_part.shape[0]
    span = math.gcd(count, 512)
    grouped_refs = ref_part.reshape(count // span, span, width)
    grouped_labels = label_part.reshape(count // span, span, classes)

    def advance(current, members):
        return (absorb(current, queries, members[0], members[1], score_scale), None)

    running, _ = lax.scan(advance, running, (grouped_refs, grouped_labels))
    row_top, row_total, row_mass = running
    share = query_rows // lax.axis_size("ref")
    row_top, row_total, row_mass = merged((row_top, row_total, row_mass), "ref", combine)
    offset = lax.axis_index("ref") * share
    mass_rows = lax.dynamic_slice_in_dim(row_mass, offset, share, 0)
    total_rows = lax.dynamic_slice_in_dim(row_total, offset, share, 0)
    return jnp.log(mass_rows) - jnp.log(total_rows)[:, None]


LANES = 128
STAT_ROWS = 16
CUTS = (0, 256, 512)
GRANT = 24 << 20
BF16 = jnp.bfloat16
F32 = jnp.float32
VMEM = pl.BlockSpec(memory_space=pltpu.VMEM)
SMEM = pl.BlockSpec(memory_space=pltpu.SMEM)


def call(kernel, outs, in_specs, flops):
    shapes = [jax.ShapeDtypeStruct(shape, dtype) for shape, dtype in outs]
    moved = sum(math.prod(shape) * jnp.dtype(dtype).itemsize for shape, dtype in outs)
    return pl.pallas_call(
        kernel,
        out_shape=shapes,
        in_specs=in_specs,
        out_specs=[VMEM] * len(shapes),
        cost_estimate=pl.CostEstimate(flops=flops, bytes_accessed=moved, transcendentals=0),
        compiler_params=pltpu.CompilerParams(vmem_limit_bytes=GRANT),
    )


def swapped(value, axis, bit):
    return lax.ppermute(value, axis, [(i, i ^ bit) for i in range(lax.axis_size(axis))])


def scored(ref_rows, queries):
    scale = 2.0 / math.sqrt(queries.shape[1])
    return (
        lax.dot_general(
            ref_rows, queries, (((1,), (1,)), ((), ())), preferred_element_type=F32
        )
        * scale
    )


def even_top(top):
    return top.astype(BF16).astype(F32)


def arrange_kernel(cuts, place_ref, queries_ref, labels_ref, ordered_ref, *label_refs):
    share = LANES
    place = place_ref[0]
    for first, last, label_ref in zip(cuts, cuts[1:], label_refs):
        label_ref[...] = labels_ref[:, first:last].T
    for block in range(queries_ref.shape[0] // share):
        first = pl.multiple_of((place ^ block) * share, share)
        ordered_ref[block * share : (block + 1) * share, :] = queries_ref[pl.ds(first, share), :]


def own_kernel(queries_ref, refs_a, refs_b, *refs):
    parts = (len(refs) - 1) // 3
    labels_a, labels_b, masses, stat_ref = (
        refs[:parts],
        refs[parts : 2 * parts],
        refs[2 * parts : 3 * parts],
        refs[-1],
    )
    queries = queries_ref[...]
    scores_a = scored(refs_a[...], queries)
    scores_b = scored(refs_b[...], queries)
    top = jnp.maximum(
        jnp.max(scores_a, axis=0, keepdims=True), jnp.max(scores_b, axis=0, keepdims=True)
    )
    top = even_top(top)
    weights_a = jnp.exp(scores_a - top).astype(BF16)
    weights_b = jnp.exp(scores_b - top).astype(BF16)
    total = jnp.sum(weights_a.astype(F32), axis=0, keepdims=True) + jnp.sum(
        weights_b.astype(F32), axis=0, keepdims=True
    )
    for out, first, second in zip(masses, labels_a, labels_b):
        out[...] = jnp.dot(first[...], weights_a, preferred_element_type=F32) + jnp.dot(
            second[...], weights_b, preferred_element_type=F32
        )
    stat_ref[0:1, :] = top
    stat_ref[1:2, :] = total


def score_kernel(queries_ref, refs_ref, scores_ref):
    scores_ref[...] = scored(refs_ref[...], queries_ref[...])


def weight_kernel(queries_ref, refs_ref, scores_ref, stat_ref, weights_ref, out_ref):
    scores_a = scores_ref[...]
    scores_b = scored(refs_ref[...], queries_ref[...])
    rows = scores_a.shape[0]
    top = jnp.maximum(
        jnp.max(scores_a, axis=0, keepdims=True), jnp.max(scores_b, axis=0, keepdims=True)
    )
    own_top = stat_ref[0:1, :]
    top = jnp.maximum(even_top(top), own_top)
    weights_a = jnp.exp(scores_a - top).astype(BF16)
    weights_b = jnp.exp(scores_b - top).astype(BF16)
    weights_ref[:rows, :] = weights_a
    weights_ref[rows:, :] = weights_b
    shrink = jnp.exp(own_top - top)
    total = (
        stat_ref[1:2, :] * shrink
        + jnp.sum(weights_a.astype(F32), axis=0, keepdims=True)
        + jnp.sum(weights_b.astype(F32), axis=0, keepdims=True)
    )
    out_ref[0:1, :] = top
    out_ref[1:2, :] = total
    out_ref[2:3, :] = shrink


def write_message(message_ref, columns, mass, top, total):
    height = mass.shape[0]
    high = total.astype(BF16)
    low = (total - high.astype(F32)).astype(BF16)
    message_ref[:height, columns] = mass.astype(BF16)
    row = lax.broadcasted_iota(jnp.int32, (STAT_ROWS, mass.shape[1]), 0)
    stats = jnp.where(
        row == 0, top, jnp.where(row == 1, high.astype(F32), low.astype(F32))
    )
    message_ref[height:, columns] = stats.astype(BF16)


def read_message(message_ref, columns):
    height = message_ref.shape[0] - STAT_ROWS
    mass = message_ref[:height, columns].astype(F32)
    stats = message_ref[height:, columns].astype(F32)
    return mass, stats[0:1], stats[1:2] + stats[2:3]


def mass_kernel(label_a, label_b, weights_ref, own_ref, stat_ref, message_ref, keep_ref):
    rows = label_a.shape[1]
    mass = (
        own_ref[...] * stat_ref[2:3, :]
        + jnp.dot(label_a[...], weights_ref[:rows, :], preferred_element_type=F32)
        + jnp.dot(label_b[...], weights_ref[rows:, :], preferred_element_type=F32)
    )
    for slot in range(2):
        columns = slice(slot * LANES, (slot + 1) * LANES)
        kept = slice(2 * slot * LANES, (2 * slot + 1) * LANES)
        sent = slice((2 * slot + 1) * LANES, (2 * slot + 2) * LANES)
        write_message(
            message_ref, columns, mass[:, sent], stat_ref[0:1, sent], stat_ref[1:2, sent]
        )
        keep_ref[:, columns] = mass[:, kept]


def joined(mass, top, total, other):
    other_mass, other_top, other_total = other
    new_top = jnp.maximum(top, other_top)
    scale = jnp.exp(top - new_top)
    other_scale = jnp.exp(other_top - new_top)
    return (
        mass * scale + other_mass * other_scale,
        new_top,
        total * scale + other_total * other_scale,
    )


def halve_kernel(received_ref, keep_ref, stat_ref, message_ref, out_ref, out_stat_ref):
    near, far = slice(0, LANES), slice(LANES, 2 * LANES)
    block = slice(2 * LANES, 3 * LANES)
    mass, top, total = joined(
        keep_ref[:, far], stat_ref[0:1, block], stat_ref[1:2, block], read_message(received_ref, far)
    )
    write_message(message_ref, slice(None), mass, top, total)
    mass, top, total = joined(
        keep_ref[:, near], stat_ref[0:1, near], stat_ref[1:2, near], read_message(received_ref, near)
    )
    out_ref[...] = mass
    out_stat_ref[0:1, :] = top
    out_stat_ref[1:2, :] = total


def final_kernel(stat_ref, *refs):
    parts = len(refs) // 2
    got, kept, out_ref = refs[:parts], refs[parts : 2 * parts], refs[-1]
    first = 0
    for message_ref, keep_ref in zip(got, kept):
        last = first + keep_ref.shape[0]
        mass, _, total = joined(
            keep_ref[...], stat_ref[0:1, :], stat_ref[1:2, :], read_message(message_ref, slice(None))
        )
        out_ref[:, first:last] = (jnp.log(mass) - jnp.log(total)).T
        first = last


def fits(queries, references, labels):
    share = queries.shape[0] // lax.axis_size("ref")
    return (
        lax.axis_size("blk") == 4
        and lax.axis_size("ref") == 4
        and share == LANES
        and labels.shape[1] % (2 * LANES) == 0
        and references.shape[0] % LANES == 0
    )


def spans(classes):
    steps = [cut * classes // 512 for cut in CUTS]
    return steps if all(cut % LANES == 0 for cut in steps) else [0, classes]


def per_device(queries, references, labels):
    if not fits(queries, references, labels):
        return plain(queries, references, labels)
    return exchanged(queries, references, labels)


def exchanged(queries, references, labels):
    count, width = references.shape
    rows, classes = queries.shape[0], labels.shape[1]
    cuts = spans(classes)
    heights = [last - first for first, last in zip(cuts, cuts[1:])]
    parts = len(heights)
    pair = 2 * LANES
    score_flops = 2 * count * rows * width
    mass_flops = [4 * count * rows * height for height in heights]

    far_refs = swapped(references, "blk", 2)
    mate_refs = swapped(references, "blk", 1)
    place = lax.axis_index("ref").astype(jnp.int32).reshape(1)
    ordered, *own_labels = call(
        functools.partial(arrange_kernel, cuts),
        [((rows, width), BF16)] + [((height, count), BF16) for height in heights],
        [SMEM, VMEM, VMEM],
        0,
    )(place, queries, labels)
    far_labels = [swapped(part, "blk", 2) for part in own_labels]
    mate_labels = [swapped(part, "blk", 1) for part in own_labels]
    *own_masses, own_stat = call(
        own_kernel,
        [((height, rows), F32) for height in heights] + [((8, rows), F32)],
        [VMEM] * (3 + 2 * parts),
        2 * score_flops + 2 * sum(mass_flops),
    )(ordered, references, mate_refs, *own_labels, *mate_labels)
    cross_refs = swapped(far_refs, "blk", 1)
    cross_labels = [swapped(part, "blk", 1) for part in far_labels]
    (scores,) = call(
        score_kernel, [((count, rows), F32)], [VMEM] * 2, score_flops
    )(ordered, far_refs)
    weights, stat = call(
        weight_kernel, [((2 * count, rows), BF16), ((8, rows), F32)], [VMEM] * 4, score_flops
    )(ordered, cross_refs, scores, own_stat)
    got, kept = [], []
    for i in range(parts):
        height = heights[i]
        message, keep = call(
            mass_kernel,
            [((height + STAT_ROWS, pair), BF16), ((height, pair), F32)],
            [VMEM] * 5,
            mass_flops[i],
        )(far_labels[i], cross_labels[i], weights, own_masses[i], stat)
        received = swapped(message, "ref", 1)
        message, keep, near_stat = call(
            halve_kernel,
            [((height + STAT_ROWS, LANES), BF16), ((height, LANES), F32), ((8, LANES), F32)],
            [VMEM] * 3,
            0,
        )(received, keep, stat)
        got.append(swapped(message, "ref", 2))
        kept.append(keep)
    (out,) = call(final_kernel, [((LANES, classes), F32)], [VMEM] * (1 + 2 * parts), 0)(
        near_stat, *got, *kept
    )
    return out


def solution(mesh):
    return jax.shard_map(
        per_device,
        mesh=mesh,
        in_specs=(
            P(("groups", "blk"), None),
            P(("groups", "blk", "ref"), None),
            P(("groups", "blk", "ref"), None),
        ),
        out_specs=P(("groups", "blk", "ref"), None),
        check_vma=False,
    )
```

```python
import functools
import math

import jax
import jax.numpy as jnp
from jax import lax
from jax.experimental import pallas as pl
from jax.experimental.pallas import tpu as pltpu
from jax.sharding import PartitionSpec as P


NEG_FLOOR = -1e30


def merged(value, axis, join):
    pieces = jax.tree.map(lambda part: lax.all_gather(part, axis), value)
    head = jax.tree.map(lambda part: part[0], pieces)
    tail = jax.tree.map(lambda part: part[1:], pieces)
    subtotal, _ = lax.scan(lambda subtotal, piece: (join(subtotal, piece), None), head, tail)
    return subtotal


def absorb(running, queries, ref_rows, label_rows, score_scale):
    row_top, row_total, row_mass = running
    scores = (
        lax.dot_general(
            queries, ref_rows, (((1,), (1,)), ((), ())), preferred_element_type=jnp.float32
        )
        * score_scale
    )
    new_top = jnp.maximum(row_top, jnp.max(scores, axis=1))
    shrink = jnp.exp(row_top - new_top)
    weights = jnp.exp(scores - new_top[:, None]).astype(jnp.bfloat16)
    row_total = row_total * shrink + jnp.sum(weights.astype(jnp.float32), axis=1)
    row_mass = row_mass * shrink[:, None] + jnp.dot(
        weights, label_rows, preferred_element_type=jnp.float32
    )
    return (new_top, row_total, row_mass)


def combine(first, second):
    new_top = jnp.maximum(first[0], second[0])
    scale_first = jnp.exp(first[0] - new_top)
    scale_second = jnp.exp(second[0] - new_top)
    row_total = first[1] * scale_first + second[1] * scale_second
    row_mass = first[2] * scale_first[:, None] + second[2] * scale_second[:, None]
    return (new_top, row_total, row_mass)


def plain(queries, references, labels):
    width = queries.shape[1]
    classes = labels.shape[1]
    query_rows = queries.shape[0]
    score_scale = 2.0 / math.sqrt(width)
    initial = (
        jnp.full((query_rows,), NEG_FLOOR, jnp.float32),
        jnp.zeros((query_rows,), jnp.float32),
        jnp.zeros((query_rows, classes), jnp.float32),
    )
    running = initial
    ref_part = lax.all_gather(references, "blk", axis=0, tiled=True)
    label_part = lax.all_gather(labels, "blk", axis=0, tiled=True)
    count = ref_part.shape[0]
    span = math.gcd(count, 512)
    grouped_refs = ref_part.reshape(count // span, span, width)
    grouped_labels = label_part.reshape(count // span, span, classes)

    def advance(current, members):
        return (absorb(current, queries, members[0], members[1], score_scale), None)

    running, _ = lax.scan(advance, running, (grouped_refs, grouped_labels))
    row_top, row_total, row_mass = running
    share = query_rows // lax.axis_size("ref")
    row_top, row_total, row_mass = merged((row_top, row_total, row_mass), "ref", combine)
    offset = lax.axis_index("ref") * share
    mass_rows = lax.dynamic_slice_in_dim(row_mass, offset, share, 0)
    total_rows = lax.dynamic_slice_in_dim(row_total, offset, share, 0)
    return jnp.log(mass_rows) - jnp.log(total_rows)[:, None]


LANES = 128
STAT_ROWS = 16
CUTS = (0, 256, 512)
GRANT = 24 << 20
BF16 = jnp.bfloat16
F32 = jnp.float32
VMEM = pl.BlockSpec(memory_space=pltpu.VMEM)
SMEM = pl.BlockSpec(memory_space=pltpu.SMEM)


def call(kernel, outs, in_specs, flops):
    shapes = [jax.ShapeDtypeStruct(shape, dtype) for shape, dtype in outs]
    moved = sum(math.prod(shape) * jnp.dtype(dtype).itemsize for shape, dtype in outs)
    return pl.pallas_call(
        kernel,
        out_shape=shapes,
        in_specs=in_specs,
        out_specs=[VMEM] * len(shapes),
        cost_estimate=pl.CostEstimate(flops=flops, bytes_accessed=moved, transcendentals=0),
        compiler_params=pltpu.CompilerParams(vmem_limit_bytes=GRANT),
    )


def swapped(value, axis, bit):
    return lax.ppermute(value, axis, [(i, i ^ bit) for i in range(lax.axis_size(axis))])


def scored(ref_rows, queries):
    scale = 2.0 / math.sqrt(queries.shape[1])
    return (
        lax.dot_general(
            ref_rows, queries, (((1,), (1,)), ((), ())), preferred_element_type=F32
        )
        * scale
    )


def even_top(top):
    return top.astype(BF16).astype(F32)


def arrange_kernel(cuts, place_ref, queries_ref, labels_ref, ordered_ref, *label_refs):
    share = LANES
    place = place_ref[0]
    for first, last, label_ref in zip(cuts, cuts[1:], label_refs):
        label_ref[...] = labels_ref[:, first:last].T
    for block in range(queries_ref.shape[0] // share):
        first = pl.multiple_of((place ^ block) * share, share)
        ordered_ref[block * share : (block + 1) * share, :] = queries_ref[pl.ds(first, share), :]


def own_kernel(queries_ref, refs_a, refs_b, *refs):
    parts = (len(refs) - 1) // 3
    labels_a, labels_b, masses, stat_ref = (
        refs[:parts],
        refs[parts : 2 * parts],
        refs[2 * parts : 3 * parts],
        refs[-1],
    )
    queries = queries_ref[...]
    scores_a = scored(refs_a[...], queries)
    scores_b = scored(refs_b[...], queries)
    top = jnp.maximum(
        jnp.max(scores_a, axis=0, keepdims=True), jnp.max(scores_b, axis=0, keepdims=True)
    )
    top = even_top(top)
    weights_a = jnp.exp(scores_a - top).astype(BF16)
    weights_b = jnp.exp(scores_b - top).astype(BF16)
    total = jnp.sum(weights_a.astype(F32), axis=0, keepdims=True) + jnp.sum(
        weights_b.astype(F32), axis=0, keepdims=True
    )
    for out, first, second in zip(masses, labels_a, labels_b):
        out[...] = jnp.dot(first[...], weights_a, preferred_element_type=F32) + jnp.dot(
            second[...], weights_b, preferred_element_type=F32
        )
    stat_ref[0:1, :] = top
    stat_ref[1:2, :] = total


def far_kernel(queries_ref, refs_ref, stat_ref, weights_ref, out_ref):
    scores = scored(refs_ref[...], queries_ref[...])
    old_top = stat_ref[0:1, :]
    top = jnp.maximum(even_top(jnp.max(scores, axis=0, keepdims=True)), old_top)
    weights = jnp.exp(scores - top).astype(BF16)
    weights_ref[...] = weights
    shrink = jnp.exp(old_top - top)
    total = stat_ref[1:2, :] * shrink + jnp.sum(weights.astype(F32), axis=0, keepdims=True)
    out_ref[0:1, :] = top
    out_ref[1:2, :] = total
    out_ref[2:3, :] = shrink


def write_stats(message_ref, height, top, total):
    high = total.astype(BF16)
    low = (total - high.astype(F32)).astype(BF16)
    row = lax.broadcasted_iota(jnp.int32, (STAT_ROWS, total.shape[1]), 0)
    stats = jnp.where(row == 0, top, jnp.where(row == 1, high.astype(F32), low.astype(F32)))
    message_ref[height:, :] = stats.astype(BF16)


def write_message(message_ref, mass, top, total):
    height = mass.shape[0]
    message_ref[:height, :] = mass.astype(BF16)
    write_stats(message_ref, height, top, total)


def read_message(message_ref, first=0, last=None):
    height = message_ref.shape[0] - STAT_ROWS
    mass = message_ref[first : last or height, :].astype(F32)
    stats = message_ref[height:, :].astype(F32)
    return mass, stats[0:1], stats[1:2] + stats[2:3]


def cross_mass(far_labels, cross_labels, far_weights, cross_weights, own_ref, far_stat, stat_ref):
    mass = own_ref[...] * far_stat[2:3, :] + jnp.dot(
        far_labels[...], far_weights[...], preferred_element_type=F32
    )
    return mass * stat_ref[2:3, :] + jnp.dot(
        cross_labels[...], cross_weights[...], preferred_element_type=F32
    )


def block_of(index):
    return slice(index * LANES, (index + 1) * LANES)


def mass_kernel(*refs):
    stat_ref, earlier, (far_ref, near_ref, middle_ref, keep_ref) = refs[6], refs[7:-4], refs[-4:]
    mass = cross_mass(*refs[:7])
    sent = block_of(3)
    write_message(far_ref, mass[:, sent], stat_ref[0:1, sent], stat_ref[1:2, sent])
    middle_ref[...] = mass[:, block_of(2)]
    keep_ref[...] = mass[:, block_of(0)]
    first = 0
    for piece_ref in earlier:
        near_ref[: piece_ref.shape[0], :] = piece_ref[...]
        first = piece_ref.shape[0]
    last = first + mass.shape[0]
    near_ref[first:last, :] = mass[:, block_of(1)].astype(BF16)
    if near_ref.shape[0] > last:
        write_stats(near_ref, last, stat_ref[0:1, block_of(1)], stat_ref[1:2, block_of(1)])


def joined(mass, top, total, other):
    other_mass, other_top, other_total = other
    new_top = jnp.maximum(top, other_top)
    scale = jnp.exp(top - new_top)
    other_scale = jnp.exp(other_top - new_top)
    return (
        mass * scale + other_mass * other_scale,
        new_top,
        total * scale + other_total * other_scale,
    )


def halve_kernel(received_ref, middle_ref, stat_ref, message_ref):
    block = block_of(2)
    write_message(
        message_ref,
        *joined(
            middle_ref[...],
            stat_ref[0:1, block],
            stat_ref[1:2, block],
            read_message(received_ref),
        ),
    )


def logged(mass, top, total):
    return (jnp.log(mass) - jnp.log(total)).T


def early_kernel(near_ref, last_ref, keep_a, keep_b, stat_ref, out_ref, mass_ref, out_stat_ref):
    top, total = stat_ref[0:1, block_of(0)], stat_ref[1:2, block_of(0)]
    cut = keep_a.shape[0]
    part = joined(keep_a[...], top, total, read_message(near_ref, 0, cut))
    out_ref[...] = logged(*joined(*part, read_message(last_ref)))
    mass, top, total = joined(keep_b[...], top, total, read_message(near_ref, cut))
    mass_ref[...] = mass
    out_stat_ref[0:1, :] = top
    out_stat_ref[1:2, :] = total


def final_kernel(early_ref, last_ref, mass_ref, stat_ref, out_ref):
    early = early_ref.shape[1]
    out_ref[:, :early] = early_ref[...]
    part = mass_ref[...], stat_ref[0:1, :], stat_ref[1:2, :]
    out_ref[:, early:] = logged(*joined(*part, read_message(last_ref)))


def fits(queries, references, labels):
    share = queries.shape[0] // lax.axis_size("ref")
    return (
        lax.axis_size("blk") == 4
        and lax.axis_size("ref") == 4
        and share == LANES
        and labels.shape[1] % (2 * LANES) == 0
        and references.shape[0] % LANES == 0
    )


def spans(classes):
    steps = [cut * classes // 512 for cut in CUTS]
    return steps if all(cut % LANES == 0 for cut in steps) else [0, classes]


def per_device(queries, references, labels):
    if not fits(queries, references, labels):
        return plain(queries, references, labels)
    return exchanged(queries, references, labels)


def exchanged(queries, references, labels):
    count, width = references.shape
    rows, classes = queries.shape[0], labels.shape[1]
    cuts = spans(classes)
    heights = [last - first for first, last in zip(cuts, cuts[1:])]
    parts = len(heights)
    score_flops = 2 * count * rows * width
    mass_flops = [4 * count * rows * height for height in heights]

    far_refs = swapped(references, "blk", 2)
    mate_refs = swapped(references, "blk", 1)
    place = lax.axis_index("ref").astype(jnp.int32).reshape(1)
    ordered, *own_labels = call(
        functools.partial(arrange_kernel, cuts),
        [((rows, width), BF16)] + [((height, count), BF16) for height in heights],
        [SMEM, VMEM, VMEM],
        0,
    )(place, queries, labels)
    far_labels = [swapped(part, "blk", 2) for part in own_labels]
    mate_labels = [swapped(part, "blk", 1) for part in own_labels]
    *own_masses, own_stat = call(
        own_kernel,
        [((height, rows), F32) for height in heights] + [((8, rows), F32)],
        [VMEM] * (3 + 2 * parts),
        2 * score_flops + 2 * sum(mass_flops),
    )(ordered, references, mate_refs, *own_labels, *mate_labels)
    cross_refs = swapped(far_refs, "blk", 1)
    cross_labels = [swapped(part, "blk", 1) for part in far_labels]
    stat_shape = ((8, rows), F32)
    far_weights, far_stat = call(
        far_kernel, [((count, rows), BF16), stat_shape], [VMEM] * 3, score_flops
    )(ordered, far_refs, own_stat)
    cross_weights, stat = call(
        far_kernel, [((count, rows), BF16), stat_shape], [VMEM] * 3, score_flops
    )(ordered, cross_refs, far_stat)

    def operands(i):
        return (
            far_labels[i],
            cross_labels[i],
            far_weights,
            cross_weights,
            own_masses[i],
            far_stat,
            stat,
        )

    def message_shape(height):
        return ((height + STAT_ROWS, LANES), BF16)

    near, kept, lasts = (), [], []
    for i, height in enumerate(heights):
        sizes = [
            message_shape(height),
            message_shape(classes) if i else ((height, LANES), BF16),
            ((height, LANES), F32),
            ((height, LANES), F32),
        ]
        far, piece, middle, keep = call(
            mass_kernel, sizes, [VMEM] * (7 + len(near)), mass_flops[i]
        )(*operands(i), *near)
        near = (piece,)
        kept.append(keep)
        (message,) = call(halve_kernel, [message_shape(height)], [VMEM] * 3, 0)(
            swapped(far, "ref", 1), middle, stat
        )
        lasts.append(swapped(message, "ref", 2))
    near = swapped(*near, "ref", 1)
    early, mass, near_stat = call(
        early_kernel,
        [((LANES, heights[0]), F32), ((heights[1], LANES), F32), ((8, LANES), F32)],
        [VMEM] * 5,
        0,
    )(near, lasts[0], *kept, stat)
    (out,) = call(final_kernel, [((LANES, classes), F32)], [VMEM] * 4, 0)(
        early, lasts[1], mass, near_stat
    )
    return out


def solution(mesh):
    return jax.shard_map(
        per_device,
        mesh=mesh,
        in_specs=(
            P(("groups", "blk"), None),
            P(("groups", "blk", "ref"), None),
            P(("groups", "blk", "ref"), None),
        ),
        out_specs=P(("groups", "blk", "ref"), None),
        check_vma=False,
    )
```

```python
import functools
import math

import jax
import jax.numpy as jnp
from jax import lax
from jax.experimental import pallas as pl
from jax.experimental.pallas import tpu as pltpu
from jax.sharding import PartitionSpec as P


NEG_FLOOR = -1e30


def merged(value, axis, join):
    pieces = jax.tree.map(lambda part: lax.all_gather(part, axis), value)
    head = jax.tree.map(lambda part: part[0], pieces)
    tail = jax.tree.map(lambda part: part[1:], pieces)
    subtotal, _ = lax.scan(lambda subtotal, piece: (join(subtotal, piece), None), head, tail)
    return subtotal


def absorb(running, queries, ref_rows, label_rows, score_scale):
    row_top, row_total, row_mass = running
    scores = (
        lax.dot_general(
            queries, ref_rows, (((1,), (1,)), ((), ())), preferred_element_type=jnp.float32
        )
        * score_scale
    )
    new_top = jnp.maximum(row_top, jnp.max(scores, axis=1))
    shrink = jnp.exp(row_top - new_top)
    weights = jnp.exp(scores - new_top[:, None]).astype(jnp.bfloat16)
    row_total = row_total * shrink + jnp.sum(weights.astype(jnp.float32), axis=1)
    row_mass = row_mass * shrink[:, None] + jnp.dot(
        weights, label_rows, preferred_element_type=jnp.float32
    )
    return (new_top, row_total, row_mass)


def combine(first, second):
    new_top = jnp.maximum(first[0], second[0])
    scale_first = jnp.exp(first[0] - new_top)
    scale_second = jnp.exp(second[0] - new_top)
    row_total = first[1] * scale_first + second[1] * scale_second
    row_mass = first[2] * scale_first[:, None] + second[2] * scale_second[:, None]
    return (new_top, row_total, row_mass)


def plain(queries, references, labels):
    width = queries.shape[1]
    classes = labels.shape[1]
    query_rows = queries.shape[0]
    score_scale = 2.0 / math.sqrt(width)
    initial = (
        jnp.full((query_rows,), NEG_FLOOR, jnp.float32),
        jnp.zeros((query_rows,), jnp.float32),
        jnp.zeros((query_rows, classes), jnp.float32),
    )
    running = initial
    ref_part = lax.all_gather(references, "blk", axis=0, tiled=True)
    label_part = lax.all_gather(labels, "blk", axis=0, tiled=True)
    count = ref_part.shape[0]
    span = math.gcd(count, 512)
    grouped_refs = ref_part.reshape(count // span, span, width)
    grouped_labels = label_part.reshape(count // span, span, classes)

    def advance(current, members):
        return (absorb(current, queries, members[0], members[1], score_scale), None)

    running, _ = lax.scan(advance, running, (grouped_refs, grouped_labels))
    row_top, row_total, row_mass = running
    share = query_rows // lax.axis_size("ref")
    row_top, row_total, row_mass = merged((row_top, row_total, row_mass), "ref", combine)
    offset = lax.axis_index("ref") * share
    mass_rows = lax.dynamic_slice_in_dim(row_mass, offset, share, 0)
    total_rows = lax.dynamic_slice_in_dim(row_total, offset, share, 0)
    return jnp.log(mass_rows) - jnp.log(total_rows)[:, None]


LANES = 128
STAT_ROWS = 16
CUTS = (0, 256, 512)
GRANT = 24 << 20
BF16 = jnp.bfloat16
F32 = jnp.float32
VMEM = pl.BlockSpec(memory_space=pltpu.VMEM)
SMEM = pl.BlockSpec(memory_space=pltpu.SMEM)


def call(kernel, outs, in_specs, flops):
    shapes = [jax.ShapeDtypeStruct(shape, dtype) for shape, dtype in outs]
    moved = sum(math.prod(shape) * jnp.dtype(dtype).itemsize for shape, dtype in outs)
    return pl.pallas_call(
        kernel,
        out_shape=shapes,
        in_specs=in_specs,
        out_specs=[VMEM] * len(shapes),
        cost_estimate=pl.CostEstimate(flops=flops, bytes_accessed=moved, transcendentals=0),
        compiler_params=pltpu.CompilerParams(vmem_limit_bytes=GRANT),
    )


def swapped(value, axis, bit):
    return lax.ppermute(value, axis, [(i, i ^ bit) for i in range(lax.axis_size(axis))])


def scored(ref_rows, queries):
    scale = 2.0 / math.sqrt(queries.shape[1])
    return (
        lax.dot_general(
            ref_rows, queries, (((1,), (1,)), ((), ())), preferred_element_type=F32
        )
        * scale
    )


def even_top(top):
    return top.astype(BF16).astype(F32)


def arrange_kernel(cuts, place_ref, queries_ref, labels_ref, ordered_ref, *label_refs):
    share = LANES
    place = place_ref[0]
    for first, last, label_ref in zip(cuts, cuts[1:], label_refs):
        label_ref[...] = labels_ref[:, first:last].T
    for block in range(queries_ref.shape[0] // share):
        first = pl.multiple_of((place ^ block) * share, share)
        ordered_ref[block * share : (block + 1) * share, :] = queries_ref[pl.ds(first, share), :]


def own_kernel(queries_ref, refs_a, refs_b, *refs):
    parts = (len(refs) - 1) // 3
    labels_a, labels_b, masses, stat_ref = (
        refs[:parts],
        refs[parts : 2 * parts],
        refs[2 * parts : 3 * parts],
        refs[-1],
    )
    queries = queries_ref[...]
    scores_a = scored(refs_a[...], queries)
    scores_b = scored(refs_b[...], queries)
    top = jnp.maximum(
        jnp.max(scores_a, axis=0, keepdims=True), jnp.max(scores_b, axis=0, keepdims=True)
    )
    top = even_top(top)
    weights_a = jnp.exp(scores_a - top).astype(BF16)
    weights_b = jnp.exp(scores_b - top).astype(BF16)
    total = jnp.sum(weights_a.astype(F32), axis=0, keepdims=True) + jnp.sum(
        weights_b.astype(F32), axis=0, keepdims=True
    )
    for out, first, second in zip(masses, labels_a, labels_b):
        out[...] = jnp.dot(first[...], weights_a, preferred_element_type=F32) + jnp.dot(
            second[...], weights_b, preferred_element_type=F32
        )
    stat_ref[0:1, :] = top
    stat_ref[1:2, :] = total


def far_kernel(queries_ref, refs_ref, stat_ref, weights_ref, out_ref):
    scores = scored(refs_ref[...], queries_ref[...])
    old_top = stat_ref[0:1, :]
    top = jnp.maximum(even_top(jnp.max(scores, axis=0, keepdims=True)), old_top)
    weights = jnp.exp(scores - top).astype(BF16)
    weights_ref[...] = weights
    shrink = jnp.exp(old_top - top)
    total = stat_ref[1:2, :] * shrink + jnp.sum(weights.astype(F32), axis=0, keepdims=True)
    out_ref[0:1, :] = top
    out_ref[1:2, :] = total
    out_ref[2:3, :] = shrink


def halves_of(value):
    high = value.astype(BF16).astype(F32)
    return high, (value - high).astype(BF16).astype(F32)


def center_of(mass):
    least = jnp.min(mass, axis=0, keepdims=True)
    return halves_of(jnp.minimum(jnp.mean(mass, axis=0, keepdims=True), 2.0 * least))


def write_message(message_ref, mass, top, total):
    height = mass.shape[0]
    rows = (top, *halves_of(total), *center_of(mass))
    message_ref[:height, :] = (mass - (rows[3] + rows[4])).astype(BF16)
    index = lax.broadcasted_iota(jnp.int32, (STAT_ROWS, mass.shape[1]), 0)
    stats = rows[-1]
    for row in range(len(rows) - 1):
        stats = jnp.where(index == row, rows[row], stats)
    message_ref[height:, :] = stats.astype(BF16)


def read_message(message_ref, first=0, last=None, row=3):
    stats = message_ref[message_ref.shape[0] - STAT_ROWS :, :].astype(F32)
    mass = message_ref[first : last or message_ref.shape[0] - STAT_ROWS, :].astype(F32)
    center = stats[row : row + 1] + stats[row + 1 : row + 2]
    return mass + center, stats[0:1], stats[1:2] + stats[2:3]


def cross_mass(far_labels, cross_labels, far_weights, cross_weights, own_ref, far_stat, stat_ref):
    mass = own_ref[...] * far_stat[2:3, :] + jnp.dot(
        far_labels[...], far_weights[...], preferred_element_type=F32
    )
    return mass * stat_ref[2:3, :] + jnp.dot(
        cross_labels[...], cross_weights[...], preferred_element_type=F32
    )


def block_of(index):
    return slice(index * LANES, (index + 1) * LANES)


def mass_kernel(*refs):
    stat_ref, earlier, (far_ref, near_ref, middle_ref, keep_ref) = refs[6], refs[7:-4], refs[-4:]
    mass = cross_mass(*refs[:7])
    sent, near = block_of(3), block_of(1)
    write_message(far_ref, mass[:, sent], stat_ref[0:1, sent], stat_ref[1:2, sent])
    middle_ref[...] = mass[:, block_of(2)]
    keep_ref[...] = mass[:, block_of(0)]
    if not earlier:
        write_message(near_ref, mass[:, near], stat_ref[0:1, near], stat_ref[1:2, near])
    for piece_ref in earlier:
        first = piece_ref.shape[0] - STAT_ROWS
        last = first + mass.shape[0]
        high, low = center_of(mass[:, near])
        near_ref[:first, :] = piece_ref[:first, :]
        near_ref[first:last, :] = (mass[:, near] - (high + low)).astype(BF16)
        index = lax.broadcasted_iota(jnp.int32, (STAT_ROWS, LANES), 0)
        stats = jnp.where(index == 5, high, jnp.where(index > 5, low, piece_ref[first:, :].astype(F32)))
        near_ref[last:, :] = stats.astype(BF16)


def joined(mass, top, total, other):
    other_mass, other_top, other_total = other
    new_top = jnp.maximum(top, other_top)
    scale = jnp.exp(top - new_top)
    other_scale = jnp.exp(other_top - new_top)
    return (
        mass * scale + other_mass * other_scale,
        new_top,
        total * scale + other_total * other_scale,
    )


def halve_kernel(received_ref, middle_ref, stat_ref, message_ref):
    block = block_of(2)
    write_message(
        message_ref,
        *joined(
            middle_ref[...],
            stat_ref[0:1, block],
            stat_ref[1:2, block],
            read_message(received_ref),
        ),
    )


def logged(mass, top, total):
    return (jnp.log(mass) - jnp.log(total)).T


def early_kernel(near_ref, last_ref, keep_a, keep_b, stat_ref, out_ref, mass_ref, out_stat_ref):
    top, total = stat_ref[0:1, block_of(0)], stat_ref[1:2, block_of(0)]
    cut = keep_a.shape[0]
    part = joined(keep_a[...], top, total, read_message(near_ref, 0, cut))
    out_ref[...] = logged(*joined(*part, read_message(last_ref)))
    mass, top, total = joined(keep_b[...], top, total, read_message(near_ref, cut, None, 5))
    mass_ref[...] = mass
    out_stat_ref[0:1, :] = top
    out_stat_ref[1:2, :] = total


def final_kernel(early_ref, last_ref, mass_ref, stat_ref, out_ref):
    early = early_ref.shape[1]
    out_ref[:, :early] = early_ref[...]
    part = mass_ref[...], stat_ref[0:1, :], stat_ref[1:2, :]
    out_ref[:, early:] = logged(*joined(*part, read_message(last_ref)))


def fits(queries, references, labels):
    share = queries.shape[0] // lax.axis_size("ref")
    return (
        lax.axis_size("blk") == 4
        and lax.axis_size("ref") == 4
        and share == LANES
        and labels.shape[1] % (2 * LANES) == 0
        and references.shape[0] % LANES == 0
    )


def spans(classes):
    steps = [cut * classes // 512 for cut in CUTS]
    return steps if all(cut % LANES == 0 for cut in steps) else [0, classes]


def per_device(queries, references, labels):
    if not fits(queries, references, labels):
        return plain(queries, references, labels)
    return exchanged(queries, references, labels)


def exchanged(queries, references, labels):
    count, width = references.shape
    rows, classes = queries.shape[0], labels.shape[1]
    cuts = spans(classes)
    heights = [last - first for first, last in zip(cuts, cuts[1:])]
    parts = len(heights)
    score_flops = 2 * count * rows * width
    mass_flops = [4 * count * rows * height for height in heights]

    far_refs = swapped(references, "blk", 2)
    mate_refs = swapped(references, "blk", 1)
    place = lax.axis_index("ref").astype(jnp.int32).reshape(1)
    ordered, *own_labels = call(
        functools.partial(arrange_kernel, cuts),
        [((rows, width), BF16)] + [((height, count), BF16) for height in heights],
        [SMEM, VMEM, VMEM],
        0,
    )(place, queries, labels)
    far_labels = [swapped(part, "blk", 2) for part in own_labels]
    mate_labels = [swapped(part, "blk", 1) for part in own_labels]
    *own_masses, own_stat = call(
        own_kernel,
        [((height, rows), F32) for height in heights] + [((8, rows), F32)],
        [VMEM] * (3 + 2 * parts),
        2 * score_flops + 2 * sum(mass_flops),
    )(ordered, references, mate_refs, *own_labels, *mate_labels)
    cross_refs = swapped(far_refs, "blk", 1)
    cross_labels = [swapped(part, "blk", 1) for part in far_labels]
    stat_shape = ((8, rows), F32)
    far_weights, far_stat = call(
        far_kernel, [((count, rows), BF16), stat_shape], [VMEM] * 3, score_flops
    )(ordered, far_refs, own_stat)
    cross_weights, stat = call(
        far_kernel, [((count, rows), BF16), stat_shape], [VMEM] * 3, score_flops
    )(ordered, cross_refs, far_stat)

    def operands(i):
        return (
            far_labels[i],
            cross_labels[i],
            far_weights,
            cross_weights,
            own_masses[i],
            far_stat,
            stat,
        )

    def message_shape(height):
        return ((height + STAT_ROWS, LANES), BF16)

    near, kept, lasts = (), [], []
    for i, height in enumerate(heights):
        sizes = [
            message_shape(height),
            message_shape(classes if i else height),
            ((height, LANES), F32),
            ((height, LANES), F32),
        ]
        far, piece, middle, keep = call(
            mass_kernel, sizes, [VMEM] * (7 + len(near)), mass_flops[i]
        )(*operands(i), *near)
        near = (piece,)
        kept.append(keep)
        (message,) = call(halve_kernel, [message_shape(height)], [VMEM] * 3, 0)(
            swapped(far, "ref", 1), middle, stat
        )
        lasts.append(swapped(message, "ref", 2))
    near = swapped(*near, "ref", 1)
    early, mass, near_stat = call(
        early_kernel,
        [((LANES, heights[0]), F32), ((heights[1], LANES), F32), ((8, LANES), F32)],
        [VMEM] * 5,
        0,
    )(near, lasts[0], *kept, stat)
    (out,) = call(final_kernel, [((LANES, classes), F32)], [VMEM] * 4, 0)(
        early, lasts[1], mass, near_stat
    )
    return out


def solution(mesh):
    return jax.shard_map(
        per_device,
        mesh=mesh,
        in_specs=(
            P(("groups", "blk"), None),
            P(("groups", "blk", "ref"), None),
            P(("groups", "blk", "ref"), None),
        ),
        out_specs=P(("groups", "blk", "ref"), None),
        check_vma=False,
    )
```

```python
import functools
import math

import jax
import jax.numpy as jnp
from jax import lax
from jax.experimental import pallas as pl
from jax.experimental.pallas import tpu as pltpu
from jax.sharding import PartitionSpec as P


NEG_FLOOR = -1e30


def merged(value, axis, join):
    pieces = jax.tree.map(lambda part: lax.all_gather(part, axis), value)
    head = jax.tree.map(lambda part: part[0], pieces)
    tail = jax.tree.map(lambda part: part[1:], pieces)
    subtotal, _ = lax.scan(lambda subtotal, piece: (join(subtotal, piece), None), head, tail)
    return subtotal


def absorb(running, queries, ref_rows, label_rows, score_scale):
    row_top, row_total, row_mass = running
    scores = (
        lax.dot_general(
            queries, ref_rows, (((1,), (1,)), ((), ())), preferred_element_type=jnp.float32
        )
        * score_scale
    )
    new_top = jnp.maximum(row_top, jnp.max(scores, axis=1))
    shrink = jnp.exp(row_top - new_top)
    weights = jnp.exp(scores - new_top[:, None]).astype(jnp.bfloat16)
    row_total = row_total * shrink + jnp.sum(weights.astype(jnp.float32), axis=1)
    row_mass = row_mass * shrink[:, None] + jnp.dot(
        weights, label_rows, preferred_element_type=jnp.float32
    )
    return (new_top, row_total, row_mass)


def combine(first, second):
    new_top = jnp.maximum(first[0], second[0])
    scale_first = jnp.exp(first[0] - new_top)
    scale_second = jnp.exp(second[0] - new_top)
    row_total = first[1] * scale_first + second[1] * scale_second
    row_mass = first[2] * scale_first[:, None] + second[2] * scale_second[:, None]
    return (new_top, row_total, row_mass)


def plain(queries, references, labels):
    width = queries.shape[1]
    classes = labels.shape[1]
    query_rows = queries.shape[0]
    score_scale = 2.0 / math.sqrt(width)
    initial = (
        jnp.full((query_rows,), NEG_FLOOR, jnp.float32),
        jnp.zeros((query_rows,), jnp.float32),
        jnp.zeros((query_rows, classes), jnp.float32),
    )
    running = initial
    ref_part = lax.all_gather(references, "blk", axis=0, tiled=True)
    label_part = lax.all_gather(labels, "blk", axis=0, tiled=True)
    count = ref_part.shape[0]
    span = math.gcd(count, 512)
    grouped_refs = ref_part.reshape(count // span, span, width)
    grouped_labels = label_part.reshape(count // span, span, classes)

    def advance(current, members):
        return (absorb(current, queries, members[0], members[1], score_scale), None)

    running, _ = lax.scan(advance, running, (grouped_refs, grouped_labels))
    row_top, row_total, row_mass = running
    share = query_rows // lax.axis_size("ref")
    row_top, row_total, row_mass = merged((row_top, row_total, row_mass), "ref", combine)
    offset = lax.axis_index("ref") * share
    mass_rows = lax.dynamic_slice_in_dim(row_mass, offset, share, 0)
    total_rows = lax.dynamic_slice_in_dim(row_total, offset, share, 0)
    return jnp.log(mass_rows) - jnp.log(total_rows)[:, None]


LANES = 128
STAT_ROWS = 16
CUTS = (0, 256, 512)
GRANT = 24 << 20
BF16 = jnp.bfloat16
F32 = jnp.float32
VMEM = pl.BlockSpec(memory_space=pltpu.VMEM)
SMEM = pl.BlockSpec(memory_space=pltpu.SMEM)


def call(kernel, outs, in_specs, flops, out_space=VMEM, scratch=()):
    shapes = [jax.ShapeDtypeStruct(shape, dtype) for shape, dtype in outs]
    moved = sum(math.prod(shape) * jnp.dtype(dtype).itemsize for shape, dtype in outs)
    return pl.pallas_call(
        kernel,
        out_shape=shapes,
        in_specs=in_specs,
        out_specs=[out_space] * len(shapes),
        scratch_shapes=scratch,
        cost_estimate=pl.CostEstimate(flops=flops, bytes_accessed=moved, transcendentals=0),
        compiler_params=pltpu.CompilerParams(vmem_limit_bytes=GRANT),
    )


def swapped(value, axis, bit):
    return lax.ppermute(value, axis, [(i, i ^ bit) for i in range(lax.axis_size(axis))])


def scored(ref_rows, queries):
    scale = 2.0 / math.sqrt(queries.shape[1])
    return (
        lax.dot_general(
            ref_rows, queries, (((1,), (1,)), ((), ())), preferred_element_type=F32
        )
        * scale
    )


def even_top(top):
    return top.astype(BF16).astype(F32)


def arrange_kernel(cuts, place_ref, queries_ref, labels_ref, ordered_ref, *label_refs):
    share = LANES
    place = place_ref[0]
    for first, last, label_ref in zip(cuts, cuts[1:], label_refs):
        label_ref[...] = labels_ref[:, first:last].T
    for block in range(queries_ref.shape[0] // share):
        first = pl.multiple_of((place ^ block) * share, share)
        ordered_ref[block * share : (block + 1) * share, :] = queries_ref[pl.ds(first, share), :]


def own_kernel(queries_ref, refs_a, refs_b, *refs):
    parts = (len(refs) - 1) // 3
    labels_a, labels_b, masses, stat_ref = (
        refs[:parts],
        refs[parts : 2 * parts],
        refs[2 * parts : 3 * parts],
        refs[-1],
    )
    queries = queries_ref[...]
    scores_a = scored(refs_a[...], queries)
    scores_b = scored(refs_b[...], queries)
    top = jnp.maximum(
        jnp.max(scores_a, axis=0, keepdims=True), jnp.max(scores_b, axis=0, keepdims=True)
    )
    top = even_top(top)
    weights_a = jnp.exp(scores_a - top).astype(BF16)
    weights_b = jnp.exp(scores_b - top).astype(BF16)
    total = jnp.sum(weights_a.astype(F32), axis=0, keepdims=True) + jnp.sum(
        weights_b.astype(F32), axis=0, keepdims=True
    )
    for out, first, second in zip(masses, labels_a, labels_b):
        out[...] = jnp.dot(first[...], weights_a, preferred_element_type=F32) + jnp.dot(
            second[...], weights_b, preferred_element_type=F32
        )
    stat_ref[0:1, :] = top
    stat_ref[1:2, :] = total


def far_kernel(queries_ref, refs_ref, stat_ref, weights_ref, out_ref):
    scores = scored(refs_ref[...], queries_ref[...])
    old_top = stat_ref[0:1, :]
    top = jnp.maximum(even_top(jnp.max(scores, axis=0, keepdims=True)), old_top)
    weights = jnp.exp(scores - top).astype(BF16)
    weights_ref[...] = weights
    shrink = jnp.exp(old_top - top)
    total = stat_ref[1:2, :] * shrink + jnp.sum(weights.astype(F32), axis=0, keepdims=True)
    out_ref[0:1, :] = top
    out_ref[1:2, :] = total
    out_ref[2:3, :] = shrink


def halves_of(value):
    high = value.astype(BF16).astype(F32)
    return high, (value - high).astype(BF16).astype(F32)


def center_of(mass):
    least = jnp.min(mass, axis=0, keepdims=True)
    return halves_of(jnp.minimum(jnp.mean(mass, axis=0, keepdims=True), 2.0 * least))


def write_message(message_ref, mass, top, total):
    height = mass.shape[0]
    rows = (top, *halves_of(total), *center_of(mass))
    message_ref[:height, :] = (mass - (rows[3] + rows[4])).astype(BF16)
    index = lax.broadcasted_iota(jnp.int32, (STAT_ROWS, mass.shape[1]), 0)
    stats = rows[-1]
    for row in range(len(rows) - 1):
        stats = jnp.where(index == row, rows[row], stats)
    message_ref[height:, :] = stats.astype(BF16)


def read_message(message_ref, first=0, last=None, row=3):
    stats = message_ref[message_ref.shape[0] - STAT_ROWS :, :].astype(F32)
    mass = message_ref[first : last or message_ref.shape[0] - STAT_ROWS, :].astype(F32)
    center = stats[row : row + 1] + stats[row + 1 : row + 2]
    return mass + center, stats[0:1], stats[1:2] + stats[2:3]


def cross_mass(far_labels, cross_labels, far_weights, cross_weights, own_ref, far_stat, stat_ref):
    mass = own_ref[...] * far_stat[2:3, :] + jnp.dot(
        far_labels[...], far_weights[...], preferred_element_type=F32
    )
    return mass * stat_ref[2:3, :] + jnp.dot(
        cross_labels[...], cross_weights[...], preferred_element_type=F32
    )


def block_of(index):
    return slice(index * LANES, (index + 1) * LANES)


def mass_kernel(*refs):
    stat_ref, earlier, (far_ref, near_ref, middle_ref, keep_ref) = refs[6], refs[7:-4], refs[-4:]
    mass = cross_mass(*refs[:7])
    sent, near = block_of(3), block_of(1)
    write_message(far_ref, mass[:, sent], stat_ref[0:1, sent], stat_ref[1:2, sent])
    middle_ref[...] = mass[:, block_of(2)]
    keep_ref[...] = mass[:, block_of(0)]
    if not earlier:
        write_message(near_ref, mass[:, near], stat_ref[0:1, near], stat_ref[1:2, near])
    for piece_ref in earlier:
        first = piece_ref.shape[0] - STAT_ROWS
        last = first + mass.shape[0]
        high, low = center_of(mass[:, near])
        near_ref[:first, :] = piece_ref[:first, :]
        near_ref[first:last, :] = (mass[:, near] - (high + low)).astype(BF16)
        index = lax.broadcasted_iota(jnp.int32, (STAT_ROWS, LANES), 0)
        stats = jnp.where(index == 5, high, jnp.where(index > 5, low, piece_ref[first:, :].astype(F32)))
        near_ref[last:, :] = stats.astype(BF16)


def joined(mass, top, total, other):
    other_mass, other_top, other_total = other
    new_top = jnp.maximum(top, other_top)
    scale = jnp.exp(top - new_top)
    other_scale = jnp.exp(other_top - new_top)
    return (
        mass * scale + other_mass * other_scale,
        new_top,
        total * scale + other_total * other_scale,
    )


def halve_kernel(received_ref, middle_ref, stat_ref, message_ref):
    block = block_of(2)
    write_message(
        message_ref,
        *joined(
            middle_ref[...],
            stat_ref[0:1, block],
            stat_ref[1:2, block],
            read_message(received_ref),
        ),
    )


def logged(mass, top, total):
    return (jnp.log(mass) - jnp.log(total)).T


def early_kernel(near_ref, last_ref, keep_a, keep_b, stat_ref, out_ref, mass_ref, out_stat_ref):
    top, total = stat_ref[0:1, block_of(0)], stat_ref[1:2, block_of(0)]
    cut = keep_a.shape[0]
    part = joined(keep_a[...], top, total, read_message(near_ref, 0, cut))
    out_ref[...] = logged(*joined(*part, read_message(last_ref)))
    mass, top, total = joined(keep_b[...], top, total, read_message(near_ref, cut, None, 5))
    mass_ref[...] = mass
    out_stat_ref[0:1, :] = top
    out_stat_ref[1:2, :] = total


def final_kernel(early_ref, last_ref, mass_ref, stat_ref, out_ref, late_ref, sems):
    early, late = early_ref.shape[1], late_ref.shape[1]
    ready = pltpu.make_async_copy(early_ref, out_ref.at[:, pl.ds(0, early)], sems.at[0])
    ready.start()
    part = mass_ref[...], stat_ref[0:1, :], stat_ref[1:2, :]
    late_ref[...] = logged(*joined(*part, read_message(last_ref)))
    rest = pltpu.make_async_copy(late_ref, out_ref.at[:, pl.ds(early, late)], sems.at[1])
    rest.start()
    ready.wait()
    rest.wait()


def fits(queries, references, labels):
    share = queries.shape[0] // lax.axis_size("ref")
    return (
        lax.axis_size("blk") == 4
        and lax.axis_size("ref") == 4
        and share == LANES
        and labels.shape[1] % (2 * LANES) == 0
        and references.shape[0] % LANES == 0
    )


def spans(classes):
    steps = [cut * classes // 512 for cut in CUTS]
    return steps if all(cut % LANES == 0 for cut in steps) else [0, classes]


def per_device(queries, references, labels):
    if not fits(queries, references, labels):
        return plain(queries, references, labels)
    return exchanged(queries, references, labels)


def exchanged(queries, references, labels):
    count, width = references.shape
    rows, classes = queries.shape[0], labels.shape[1]
    cuts = spans(classes)
    heights = [last - first for first, last in zip(cuts, cuts[1:])]
    parts = len(heights)
    score_flops = 2 * count * rows * width
    mass_flops = [4 * count * rows * height for height in heights]

    far_refs = swapped(references, "blk", 2)
    mate_refs = swapped(references, "blk", 1)
    place = lax.axis_index("ref").astype(jnp.int32).reshape(1)
    ordered, *own_labels = call(
        functools.partial(arrange_kernel, cuts),
        [((rows, width), BF16)] + [((height, count), BF16) for height in heights],
        [SMEM, VMEM, VMEM],
        0,
    )(place, queries, labels)
    far_labels = [swapped(part, "blk", 2) for part in own_labels]
    mate_labels = [swapped(part, "blk", 1) for part in own_labels]
    *own_masses, own_stat = call(
        own_kernel,
        [((height, rows), F32) for height in heights] + [((8, rows), F32)],
        [VMEM] * (3 + 2 * parts),
        2 * score_flops + 2 * sum(mass_flops),
    )(ordered, references, mate_refs, *own_labels, *mate_labels)
    cross_refs = swapped(far_refs, "blk", 1)
    cross_labels = [swapped(part, "blk", 1) for part in far_labels]
    stat_shape = ((8, rows), F32)
    far_weights, far_stat = call(
        far_kernel, [((count, rows), BF16), stat_shape], [VMEM] * 3, score_flops
    )(ordered, far_refs, own_stat)
    cross_weights, stat = call(
        far_kernel, [((count, rows), BF16), stat_shape], [VMEM] * 3, score_flops
    )(ordered, cross_refs, far_stat)

    def operands(i):
        return (
            far_labels[i],
            cross_labels[i],
            far_weights,
            cross_weights,
            own_masses[i],
            far_stat,
            stat,
        )

    def message_shape(height):
        return ((height + STAT_ROWS, LANES), BF16)

    near, kept, lasts = (), [], []
    for i, height in enumerate(heights):
        sizes = [
            message_shape(height),
            message_shape(classes if i else height),
            ((height, LANES), F32),
            ((height, LANES), F32),
        ]
        far, piece, middle, keep = call(
            mass_kernel, sizes, [VMEM] * (7 + len(near)), mass_flops[i]
        )(*operands(i), *near)
        near = (piece,)
        kept.append(keep)
        (message,) = call(halve_kernel, [message_shape(height)], [VMEM] * 3, 0)(
            swapped(far, "ref", 1), middle, stat
        )
        lasts.append(swapped(message, "ref", 2))
    near = swapped(*near, "ref", 1)
    early, mass, near_stat = call(
        early_kernel,
        [((LANES, heights[0]), F32), ((heights[1], LANES), F32), ((8, LANES), F32)],
        [VMEM] * 5,
        0,
    )(near, lasts[0], *kept, stat)
    (out,) = call(
        final_kernel,
        [((LANES, classes), F32)],
        [VMEM] * 4,
        0,
        pl.BlockSpec(memory_space=pltpu.HBM),
        [pltpu.VMEM((LANES, heights[1]), F32), pltpu.SemaphoreType.DMA((2,))],
    )(early, lasts[1], mass, near_stat)
    return out


def solution(mesh):
    return jax.shard_map(
        per_device,
        mesh=mesh,
        in_specs=(
            P(("groups", "blk"), None),
            P(("groups", "blk", "ref"), None),
            P(("groups", "blk", "ref"), None),
        ),
        out_specs=P(("groups", "blk", "ref"), None),
        check_vma=False,
    )
```
